128 devices in a mesh: sx: 16 (over y, x_lo, core), sy: 8 (over z, x_hi).
Axes of the slice: x: 4 (x_hi: 2, x_lo: 2; x = x_hi * 2 + x_lo), y: 4, z: 4, core: 2. Of those that a mesh axis runs over, the one named last changes fastest.
Arguments:
- adjoint_loads: float32 [16, 16, 2, 288, 128], P('sx', 'sy'), may hold values from -6 to 6
- dual_taut: bfloat16 [16, 16, 1152, 1152], P('sx', 'sy'), may hold values from -1 to 2
- dual_wrinkle: bfloat16 [16, 16, 1152, 1152], P('sx', 'sy'), may hold values from -1 to 2
- dirichlet_taut: bfloat16 [16, 16, 1152, 1152], P('sx', 'sy'), may hold values from -1 to 2
- dirichlet_wrinkle: bfloat16 [16, 16, 1152, 1152], P('sx', 'sy'), may hold values from -1 to 2
- coupling: bfloat16 [16, 16, 12, 1152], P('sx', 'sy'), may hold values from -0.25 to 0.25
- coarse_inverse: bfloat16 [896, 896], P('sx', 'sy'), may hold values from -1 to 2
- wrinkled: int32 [16, 16], P('sx', 'sy'), may hold values 0 or 1
- edge_lengths: int32 [16, 16, 2], P('sx', 'sy'), may hold values from 144 to 288
- corner_map: int32 [16, 16, 12], P('sx', 'sy'), may hold values from 0 to 895, as said below
Outputs:
- multipliers: float32 [16, 16, 2, 288, 128], P('sx', 'sy')
- preconditioned: float32 [16, 16, 2, 288, 128], P('sx', 'sy')
The draws below stay inside these ranges and needn't reach their ends.
Inputs may be any that keep to these rules, and one draw needn't show every extreme that they name: `corner_map`: each subdomain names 12 distinct coarse indices, three for each of its four grid corners; subdomains that meet at a grid corner name the same three indices for it; distinct grid corners name distinct indices.
All inputs are finite; a program needn't handle non-finite values. No bound on the sum of `wrinkled` on one device may be relied on, other than what follows from the above.
Results may differ from the reference program's by a relative error of at most 0.012.
Values may be sent and summed in bfloat16 or wider, within the bound.
No kernel may reach another device: no remote copies, remote signals or barrier semaphores. Data moves between devices by JAX's collectives and lax.ppermute only.
A program may use at most 64 MiB of HBM per device.

```python
import jax
import jax.numpy as jnp
from jax import lax

ORDER = 1152
EDGE = 288
LOADS = 128
CORNERS = 12
ITERS = 2
SUB_ROWS = 16
SUB_COLS = 16
COARSE = 896


def dominant(key, lead, size, low, high, spread_off):
    diag_key, off_key = jax.random.split(key)
    diagonal = jax.random.uniform(diag_key, lead + (size,), jnp.float32, low, high)
    off_part = jnp.clip(jax.random.normal(off_key, lead + (size, size), jnp.float32), -4.0, 4.0)
    off_part = off_part * (spread_off / size ** 0.5)
    return (off_part + jnp.eye(size, dtype=jnp.float32) * diagonal[..., None]).astype(jnp.bfloat16)


def draw_dual_taut(key, part):
    return dominant(jax.random.fold_in(key, 11), (SUB_ROWS, SUB_COLS), ORDER, 0.5, 1.5, 0.5)


def draw_dual_wrinkle(key, part):
    return dominant(jax.random.fold_in(key, 12), (SUB_ROWS, SUB_COLS), ORDER, 0.3, 0.9, 0.3)


def draw_dirichlet_taut(key, part):
    return dominant(jax.random.fold_in(key, 13), (SUB_ROWS, SUB_COLS), ORDER, 0.5, 1.5, 0.5)


def draw_dirichlet_wrinkle(key, part):
    return dominant(jax.random.fold_in(key, 14), (SUB_ROWS, SUB_COLS), ORDER, 0.3, 0.9, 0.3)


def draw_coarse_inverse(key, part):
    return dominant(jax.random.fold_in(key, 15), (), COARSE, 0.5, 1.5, 0.8)


def draw_corner_map(key, part):
    shuffled = jax.random.permutation(jax.random.fold_in(key, 21), COARSE)
    row_ids = jnp.arange(SUB_ROWS)[:, None, None]
    column_ids = jnp.arange(SUB_COLS)[None, :, None]
    slot_ids = jnp.arange(CORNERS)[None, None, :]
    corner_slot = slot_ids // 3
    down_step = jnp.array([0, 0, 1, 1])[corner_slot]
    right_step = jnp.array([0, 1, 1, 0])[corner_slot]
    grid_point = (row_ids + down_step) * (SUB_COLS + 1) + column_ids + right_step
    return shuffled[3 * grid_point + slot_ids % 3].astype(jnp.int32)


def with_ends(drawn, own_key, smallest, largest):
    extent = drawn.shape
    place = [jax.random.randint(jax.random.fold_in(own_key, axis), (), 0, extent[axis]) for axis in range(len(extent))]
    drawn = drawn.at[tuple(place)].set(smallest)
    longest = extent.index(max(extent))
    place[longest] = (place[longest] + 1) % extent[longest]
    return drawn.at[tuple(place)].set(largest)


def steps_of(key, shape, pieces, smallest, high):
    def one(dim, blocks):
        heights = jax.random.uniform(jax.random.fold_in(jax.random.fold_in(key, 6), dim), (blocks,), jnp.float32, smallest / len(pieces), high / len(pieces))
        return jnp.repeat(jnp.exp(heights), shape[dim] // blocks).reshape((-1,) + (1,) * (len(shape) - dim - 1))

    level = one(*pieces[0])
    for cut in pieces[1:]:
        level = level * one(*cut)
    return level


def normal_values(own_key, shape, deviation, bound, cuts=(), held_as=jnp.bfloat16):
    values = jax.random.normal(own_key, shape, jnp.float32) * deviation
    if len(cuts) > 0:
        values = steps_of(own_key, shape, cuts, -0.22, 0.18) * values
    return jnp.clip(values, min=-bound, max=bound).astype(held_as)


def setup_inputs(seed: int = 0) -> dict:
    key_list = jax.random.split(jax.random.key(seed), 11)
    adjoint_loads = normal_values(key_list[0], (SUB_ROWS, SUB_COLS, 2, EDGE, LOADS), 1.0, 6.0, ((0, 16), (1, 8)), jnp.float32)
    dual_taut = draw_dual_taut(jax.random.fold_in(key_list[10], 71), 0)
    dual_wrinkle = draw_dual_wrinkle(jax.random.fold_in(key_list[10], 71), 0)
    dirichlet_taut = draw_dirichlet_taut(jax.random.fold_in(key_list[10], 71), 0)
    dirichlet_wrinkle = draw_dirichlet_wrinkle(jax.random.fold_in(key_list[10], 71), 0)
    coupling = normal_values(key_list[5], (SUB_ROWS, SUB_COLS, CORNERS, ORDER), (ORDER // 2) ** -0.5, 0.25, ((0, 16), (1, 8)))
    coarse_inverse = draw_coarse_inverse(jax.random.fold_in(key_list[10], 71), 0)
    wrinkled = with_ends((jax.random.randint(key_list[7], (SUB_ROWS, SUB_COLS), 0, 3) < 1).astype(jnp.int32), jax.random.fold_in(key_list[7], 1), 0, 1)
    edge_lengths = with_ends(jax.random.randint(key_list[8], (SUB_ROWS, SUB_COLS, 2), EDGE // 2, EDGE + 1), jax.random.fold_in(key_list[8], 1), EDGE // 2, EDGE).astype(jnp.int32)
    corner_map = draw_corner_map(jax.random.fold_in(key_list[10], 71), 0)
    return {"adjoint_loads": adjoint_loads, "dual_taut": dual_taut, "dual_wrinkle": dual_wrinkle, "dirichlet_taut": dirichlet_taut, "dirichlet_wrinkle": dirichlet_wrinkle, "coupling": coupling, "coarse_inverse": coarse_inverse, "wrinkled": wrinkled, "edge_lengths": edge_lengths, "corner_map": corner_map}


step_sizes = (0.55, 0.75)
momenta = (0.0, 0.15)


def edge_mask(edge_lengths):
    positions = jnp.arange(EDGE, dtype=jnp.int32)
    inside = positions[None, None, None, :] < edge_lengths[:, :, :, None]
    row_ids = jnp.arange(SUB_ROWS, dtype=jnp.int32)[:, None] + jnp.zeros((1, SUB_COLS), jnp.int32)
    column_ids = jnp.arange(SUB_COLS, dtype=jnp.int32)[None, :] + jnp.zeros((SUB_ROWS, 1), jnp.int32)
    exists = jnp.stack([column_ids < SUB_COLS - 1, row_ids < SUB_ROWS - 1], axis=2)
    return (inside & exists[:, :, :, None]).astype(jnp.float32)[..., None]


def spread(edges):
    east_edge = edges[:, :, 0]
    south_edge = edges[:, :, 1]
    west_edge = jnp.concatenate([jnp.zeros_like(east_edge[:, :1]), east_edge[:, :-1]], axis=1)
    north_edge = jnp.concatenate([jnp.zeros_like(south_edge[:1]), south_edge[:-1]], axis=0)
    return jnp.concatenate([east_edge, south_edge, -west_edge, -north_edge], axis=2)


def collect(local_part):
    west_part = local_part[:, :, 2 * EDGE:3 * EDGE]
    right_west = jnp.concatenate([west_part[:, 1:], jnp.zeros_like(west_part[:, :1])], axis=1)
    north_part = local_part[:, :, 3 * EDGE:]
    down_north = jnp.concatenate([north_part[1:], jnp.zeros_like(north_part[:1])], axis=0)
    return jnp.stack([local_part[:, :, :EDGE] - right_west, local_part[:, :, EDGE:2 * EDGE] - down_north], axis=2)


def paired(taut, wrinkle, wrinkled, vectors):
    def one_row(operands):
        taut_row, wrinkle_row, flag_row, vector_row = operands
        vector_wide = vector_row.astype(jnp.float32)
        base_part = jnp.einsum("sij,sjl->sil", taut_row.astype(jnp.float32), vector_wide)
        extra_part = jnp.einsum("sij,sjl->sil", wrinkle_row.astype(jnp.float32), vector_wide)
        return base_part + flag_row.astype(jnp.float32)[:, None, None] * extra_part

    return lax.map(one_row, (taut, wrinkle, wrinkled, vectors))


def coarse_term(coupling, corner_map, coarse_inverse, vectors):
    coupling_wide = coupling.astype(jnp.float32)
    corner_terms = jnp.einsum("rskj,rsjl->rskl", coupling_wide, vectors.astype(jnp.float32))
    corner_index = corner_map.reshape(-1).astype(jnp.int32)
    gathered = jnp.zeros((COARSE, LOADS), jnp.float32).at[corner_index].add(corner_terms.reshape(-1, LOADS))
    solved = jnp.dot(coarse_inverse, gathered.astype(jnp.bfloat16), preferred_element_type=jnp.float32).astype(jnp.bfloat16)
    selected = solved[corner_index].reshape(SUB_ROWS, SUB_COLS, CORNERS, LOADS)
    return jnp.einsum("rskj,rskl->rsjl", coupling_wide, selected.astype(jnp.float32))


def reference(adjoint_loads, dual_taut, dual_wrinkle, dirichlet_taut, dirichlet_wrinkle, coupling, coarse_inverse, wrinkled, edge_lengths, corner_map):
    masking = edge_mask(edge_lengths)
    loads = adjoint_loads * masking

    def dual_apply(incoming):
        vectors = spread(incoming.astype(jnp.bfloat16))
        local_part = paired(dual_taut, dual_wrinkle, wrinkled, vectors)
        local_part = local_part + coarse_term(coupling, corner_map, coarse_inverse, vectors)
        return collect(local_part) * masking

    def precondition(incoming):
        vectors = spread((0.5 * incoming).astype(jnp.bfloat16))
        return 0.5 * collect(paired(dirichlet_taut, dirichlet_wrinkle, wrinkled, vectors)) * masking

    multipliers = jnp.zeros_like(loads)
    direction = jnp.zeros_like(loads)
    residual = loads
    for number in range(ITERS):
        direction = precondition(residual) + momenta[number] * direction
        multipliers = multipliers + step_sizes[number] * direction
        residual = loads - dual_apply(multipliers)
    return multipliers, precondition(residual)
```

```python
import functools

import jax
import jax.numpy as jnp
from jax import lax
from jax.experimental import pallas as pl
from jax.experimental.pallas import tpu as pltpu
from jax.sharding import PartitionSpec as P

CORNERS = 12
SLOT = 16
LANES = 128
LEN_ROWS = 16
EAST, SOUTH, WEST, NORTH = 0, 1, 2, 3
step_sizes = (0.55, 0.75)
momenta = (0.0, 0.15)


F32 = jnp.float32
BF16 = jnp.bfloat16


def shifted(shard, axis, by):
    peers = lax.axis_size(axis)
    return lax.ppermute(shard, axis, [(i, (i + by) % peers) for i in range(peers)])


def copies_of_all(shard, axis):
    peers = lax.axis_size(axis)
    return lax.all_to_all(
        jnp.broadcast_to(shard[None], (peers, *shard.shape)), axis, 0, 0, tiled=True
    )


def exchanged(outgoing):
    east, west, south, north = outgoing
    return (
        shifted(west, "sy", -1),
        shifted(east, "sy", 1),
        shifted(north, "sx", -1),
        shifted(south, "sx", 1),
    )


def dot(a, b, contract=((1,), (0,))):
    return lax.dot_general(a, b, (contract, ((), ())), preferred_element_type=F32)


def below(limit_rows, rows):
    return lax.broadcasted_iota(jnp.int32, (rows, LANES), 0).astype(F32) < limit_rows


VMEM = pl.BlockSpec(memory_space=pltpu.VMEM)
SMEM = pl.BlockSpec(memory_space=pltpu.SMEM)


def product_step(flags, taut, wrinkle, vectors, result, outgoing, rows):
    step = pl.program_id(0)
    kind, sub = step // 2, step % 2
    own = vectors[sub]
    flag = flags[sub].astype(F32)
    value = dot(taut[...], own) + flag * dot(wrinkle[...], own)
    result[sub, kind] = value
    half = value.astype(BF16)
    east, west, south, north = outgoing

    @pl.when((kind == EAST) & (sub == 1))
    def _():
        east[0, :rows] = half

    @pl.when((kind == WEST) & (sub == 0))
    def _():
        west[0, :rows] = half

    @pl.when(kind == SOUTH)
    def _():
        south[sub, :rows] = half

    @pl.when(kind == NORTH)
    def _():
        north[sub, :rows] = half


def product_call(body, flags, taut, wrinkle, others, rows, extra_rows, more_out=()):
    order = 4 * rows
    matrix = pl.BlockSpec((None, None, rows, order), lambda i: (0, i % 2, i // 2, 0))
    sent = rows + extra_rows
    whole = lambda shape: pl.BlockSpec(shape, lambda i: (0,) * len(shape))
    outs = [
        jax.ShapeDtypeStruct((2, 4, rows, LANES), F32),
        jax.ShapeDtypeStruct((1, sent, LANES), BF16),
        jax.ShapeDtypeStruct((1, sent, LANES), BF16),
        jax.ShapeDtypeStruct((2, sent, LANES), BF16),
        jax.ShapeDtypeStruct((2, sent, LANES), BF16),
        *more_out,
    ]
    return pl.pallas_call(
        body,
        out_shape=outs,
        grid=(8,),
        in_specs=[SMEM, matrix, matrix, *[whole(o.shape) for o in others]],
        out_specs=[whole(o.shape) for o in outs],
        scratch_shapes=[pltpu.VMEM((2, order, LANES), BF16)],
        compiler_params=pltpu.CompilerParams(
            dimension_semantics=("arbitrary",), vmem_limit_bytes=40 << 20
        ),
    )(flags, taut, wrinkle, *others)


def first_body(flags, taut, wrinkle, sent, from_left, from_up, pieces, own_lens,
               result, east, west, south, north, lens, vectors):
    rows = sent.shape[2] - LEN_ROWS

    @pl.when(pl.program_id(0) == 0)
    def _():
        def limit(rows_of):
            return rows_of[0:8].astype(F32) * 16.0 + rows_of[8:16].astype(F32)

        for sub in range(2):
            vectors[sub, 0 * rows : 1 * rows] = sent[sub, 0, :rows]
            vectors[sub, 1 * rows : 2 * rows] = sent[sub, 1, :rows]
            vectors[sub, 3 * rows : 4 * rows] = -from_up[sub, :rows]
            lens[sub, 0] = limit(sent[sub, 0, rows:])
            lens[sub, 1] = limit(sent[sub, 1, rows:])
            lens[sub, 3] = limit(from_up[sub, rows:])
            south[sub, rows:] = pieces[sub, SOUTH]
            north[sub, rows:] = pieces[sub, NORTH]
        vectors[0, 2 * rows : 3 * rows] = -from_left[0, :rows]
        vectors[1, 2 * rows : 3 * rows] = -sent[0, 0, :rows]
        lens[0, 2] = limit(from_left[0, rows:])
        lens[1, 2] = limit(sent[0, 0, rows:])
        east[0, rows:] = pieces[1, EAST]
        west[0, rows:] = pieces[0, WEST]

    product_step(flags, taut, wrinkle, vectors, result, (east, west, south, north), rows)


def partner(result, incoming, sub, kind, rows):
    east, west, south, north = incoming
    if kind == EAST:
        return result[1, WEST] if sub == 0 else east[0, :rows].astype(F32)
    if kind == WEST:
        return result[0, EAST] if sub == 1 else west[0, :rows].astype(F32)
    if kind == SOUTH:
        return south[sub, :rows].astype(F32)
    return north[sub, :rows].astype(F32)


def preconditioned_part(result, incoming, lens, sub, kind, rows):
    gap = result[sub, kind] - partner(result, incoming, sub, kind, rows)
    return jnp.where(below(lens[sub, kind, 0:1], rows), 0.5 * gap, 0.0)


def direction_body(number, result, east, west, south, north, lens, coupling, *rest):
    rows = result.shape[2]
    incoming = (east, west, south, north)
    if number == 0:
        kept, vectors, terms = rest
    else:
        earlier, kept, vectors, terms = rest
    for sub in range(2):
        for kind in range(4):
            part = preconditioned_part(result, incoming, lens, sub, kind, rows)
            if number == 0:
                kept[sub, kind] = part
                total = step_sizes[0] * part
            else:
                before = earlier[sub, kind]
                total = step_sizes[0] * before + step_sizes[1] * (part + momenta[1] * before)
                if kind < 2:
                    kept[sub, kind] = total
            vectors[sub, kind * rows : (kind + 1) * rows] = total.astype(BF16)
    both = vectors[...].reshape(2 * vectors.shape[1], LANES)
    terms[...] = dot(coupling[...], both).astype(BF16)


def direction_call(number, result, incoming, lens, coupling, earlier=()):
    rows = result.shape[2]
    return pl.pallas_call(
        functools.partial(direction_body, number),
        out_shape=[
            jax.ShapeDtypeStruct((2, 4 if number == 0 else 2, rows, LANES), F32),
            jax.ShapeDtypeStruct((2, 4 * rows, LANES), BF16),
            jax.ShapeDtypeStruct((2 * CORNERS, LANES), BF16),
        ],
        in_specs=[VMEM] * (7 + len(earlier)),
        out_specs=[VMEM] * 3,
        compiler_params=pltpu.CompilerParams(vmem_limit_bytes=40 << 20),
    )(result, *incoming, lens, coupling, *earlier)


def dual_body(flags, taut, wrinkle, vectors, result, east, west, south, north, unused):
    rows = result.shape[2]
    product_step(flags, taut, wrinkle, vectors, result, (east, west, south, north), rows)


def residual_body(flags, taut, wrinkle, earlier, from_east, from_west, from_south, from_north,
                  lens, terms, select, pieces, east_piece, west_piece, south_piece, north_piece,
                  loads, from_left, from_up, result, east, west, south, north, vectors):
    rows = loads.shape[2]
    incoming = (from_east, from_west, from_south, from_north)
    segments = pieces.shape[2] // SLOT

    @pl.when(pl.program_id(0) == 0)
    def _():
        solved = dot(select[...], terms[...]).astype(BF16)
        group = [solved[SLOT * k : SLOT * (k + 1)] for k in range(8)]
        other = {
            (0, EAST): (group[1], pieces[1, WEST]),
            (1, WEST): (group[0], pieces[0, EAST]),
            (0, NORTH): (group[2], north_piece[0, rows:]),
            (1, NORTH): (group[3], north_piece[1, rows:]),
            (0, SOUTH): (group[4], south_piece[0, rows:]),
            (1, SOUTH): (group[5], south_piece[1, rows:]),
            (0, WEST): (group[6], west_piece[0, rows:]),
            (1, EAST): (group[7], east_piece[0, rows:]),
        }
        for sub in range(2):
            for kind in range(4):
                values, piece = other[sub, kind]
                stacked = jnp.concatenate([group[sub], -values], axis=0)
                gap = earlier[sub, kind] - partner(earlier, incoming, sub, kind, rows)
                if kind < 2:
                    start = loads[sub, kind]
                elif kind == NORTH:
                    start = -2.0 * from_up[sub, :rows].astype(F32)
                elif sub == 1:
                    start = -loads[0, EAST]
                else:
                    start = -2.0 * from_left[0, :rows].astype(F32)
                for segment in range(segments):
                    low = segment * LANES
                    high = min(rows, low + LANES)
                    at = slice(segment * SLOT, (segment + 1) * SLOT)
                    both = jnp.concatenate([pieces[sub, kind, at], piece[at]], axis=0)
                    shift = dot(both, stacked, ((0,), (0,)))[: high - low]
                    spot = lax.broadcasted_iota(jnp.int32, (high - low, LANES), 0) + low
                    live = spot.astype(F32) < lens[sub, kind, 0:1]
                    applied = jnp.where(live, gap[low:high] + shift, 0.0)
                    vectors[sub, kind * rows + low : kind * rows + high] = (
                        0.5 * (start[low:high] - applied)
                    ).astype(BF16)

    product_step(flags, taut, wrinkle, vectors, result, (east, west, south, north), rows)


def last_body(result, east, south, lens, out):
    rows = result.shape[2]
    for sub in range(2):
        for kind in range(2):
            out[sub, kind] = preconditioned_part(
                result, (east, None, south, None), lens, sub, kind, rows
            )


def coarse_rows(coarse_inverse, corner_map):
    row_count, col_count = coarse_inverse.shape
    rows_of = lax.axis_size("sx")
    cols_of = lax.axis_size("sy")
    per = 2 * CORNERS
    row_index = lax.axis_index("sx")
    row_maps = copies_of_all(corner_map.reshape(1, per), "sy").reshape(cols_of * per)
    codes = jnp.concatenate([row_maps // 32, row_maps % 32]).astype(BF16)
    code_rows = codes.shape[0] // LANES
    tile = jnp.pad(coarse_inverse, ((0, 0), (0, LANES - col_count)))
    message = jnp.concatenate([tile, codes.reshape(code_rows, LANES)], axis=0)
    message = jnp.pad(message, ((0, 64 - message.shape[0]), (0, 0)))
    arrived = copies_of_all(message, "sx")
    columns = arrived[:, :row_count].reshape(rows_of * row_count, LANES)
    codes = arrived[:, row_count : row_count + code_rows].astype(jnp.int32)
    codes = codes.reshape(rows_of, 2, cols_of, per)
    maps = codes[:, 0] * 32 + codes[:, 1]
    at = lambda by: lax.dynamic_index_in_dim(maps, (row_index + by) % rows_of, 0, False)
    here, up, down = at(0), at(-1 + rows_of), at(1)
    groups = [
        here[:, :CORNERS],
        here[:, CORNERS:],
        up[:, :CORNERS],
        up[:, CORNERS:],
        down[:, :CORNERS],
        down[:, CORNERS:],
        jnp.roll(here, 1, axis=0)[:, CORNERS:],
        jnp.roll(here, -1, axis=0)[:, :CORNERS],
    ]
    wanted = jnp.pad(
        jnp.stack(groups, axis=1), ((0, 0), (0, 0), (0, SLOT - CORNERS)), constant_values=-1
    ).reshape(-1, 1)
    coarse_order = rows_of * row_count
    pick = (wanted == jnp.arange(coarse_order)[None]).astype(BF16)
    chosen = dot(pick, columns).astype(BF16).reshape(cols_of, -1, LANES)
    chosen = lax.all_to_all(chosen, "sy", 0, 0, tiled=True)
    flat = maps.reshape(-1)
    spot = (flat // col_count) * LANES + flat % col_count
    place = (jnp.arange(cols_of * LANES)[:, None] == spot[None]).astype(BF16)
    chosen = jnp.moveaxis(chosen, 0, 1).reshape(chosen.shape[1], -1)
    return dot(chosen, place).astype(BF16)


def local(
    adjoint_loads,
    dual_taut,
    dual_wrinkle,
    dirichlet_taut,
    dirichlet_wrinkle,
    coupling,
    coarse_inverse,
    wrinkled,
    edge_lengths,
    corner_map,
):
    rows = adjoint_loads.shape[3]
    order = 4 * rows
    loads = adjoint_loads[0]
    flags = wrinkled[0]
    columns = lax.axis_index("sy") * 2 + jnp.arange(2)
    exists = jnp.stack(
        [
            columns < 2 * lax.axis_size("sy") - 1,
            jnp.broadcast_to(lax.axis_index("sx") < lax.axis_size("sx") - 1, (2,)),
        ],
        axis=1,
    )
    own_lens = jnp.where(exists, edge_lengths[0], 0)[:, :, None, None]
    position = lax.broadcasted_iota(jnp.int32, (2, 2, rows, LANES), 2)
    loads = jnp.where(position < own_lens, loads, 0.0)
    digits = jnp.where(
        lax.broadcasted_iota(jnp.int32, (2, 2, LEN_ROWS, LANES), 2) < LEN_ROWS // 2,
        own_lens // 16,
        own_lens % 16,
    )
    sent = jnp.concatenate([(0.5 * loads).astype(BF16), digits.astype(BF16)], axis=2)
    from_left = shifted(sent[1:, 0], "sy", 1)
    from_up = shifted(sent[:, 1], "sx", 1)

    segments = -(-rows // LANES)
    pieces = coupling[0].reshape(2, CORNERS, 4, rows)
    pieces = jnp.pad(
        pieces, ((0, 0), (0, SLOT - CORNERS), (0, 0), (0, segments * LANES - rows))
    )
    pieces = pieces.reshape(2, SLOT, 4, segments, LANES)
    pieces = jnp.transpose(pieces, (0, 2, 3, 1, 4)).reshape(2, 4, segments * SLOT, LANES)
    blank = jnp.zeros((CORNERS, order), BF16)
    wide = jnp.concatenate(
        [
            jnp.concatenate([coupling[0, 0], blank], axis=1),
            jnp.concatenate([blank, coupling[0, 1]], axis=1),
        ],
        axis=0,
    )
    select = coarse_rows(coarse_inverse, corner_map)

    result, *outgoing, lens = product_call(
        first_body, flags, dirichlet_taut, dirichlet_wrinkle,
        (sent, from_left, from_up, pieces, own_lens), rows, segments * SLOT,
        (jax.ShapeDtypeStruct((2, 4, 8, LANES), F32),),
    )
    incoming = exchanged(outgoing)
    neighbour_pieces = incoming
    kept = None
    for number in range(2):
        kept, vectors, terms = direction_call(
            number, result, incoming, lens, wide, () if number == 0 else (kept,)
        )
        everyone = copies_of_all(terms, ("sx", "sy")).reshape(-1, LANES)
        result, *outgoing = product_call(
            dual_body, flags, dual_taut, dual_wrinkle, (vectors,), rows, 0
        )
        incoming = exchanged(outgoing)
        result, *outgoing = product_call(
            residual_body, flags, dirichlet_taut, dirichlet_wrinkle,
            (result, *incoming, lens, everyone, select, pieces, *neighbour_pieces,
             loads, from_left, from_up), rows, 0,
        )
        if number == 0:
            incoming = exchanged(outgoing)
    _, west, _, north = outgoing
    preconditioned = pl.pallas_call(
        last_body,
        out_shape=jax.ShapeDtypeStruct((2, 2, rows, LANES), F32),
        in_specs=[VMEM] * 4,
        out_specs=VMEM,
    )(result, shifted(west, "sy", -1), shifted(north, "sx", -1), lens)
    return kept[None], preconditioned[None]


def solution(mesh):
    placed = (
        P("sx", "sy", None, None, None),
        P("sx", "sy", None, None),
        P("sx", "sy", None, None),
        P("sx", "sy", None, None),
        P("sx", "sy", None, None),
        P("sx", "sy", None, None),
        P("sx", "sy"),
        P("sx", "sy"),
        P("sx", "sy", None),
        P("sx", "sy", None),
    )
    return jax.shard_map(
        local,
        mesh=mesh,
        in_specs=placed,
        out_specs=(P("sx", "sy", None, None, None), P("sx", "sy", None, None, None)),
        check_vma=False,
    )
```

```python
import functools

import jax
import jax.numpy as jnp
from jax import lax
from jax.experimental import pallas as pl
from jax.experimental.pallas import tpu as pltpu
from jax.sharding import PartitionSpec as P

CORNERS = 12
SLOT = 16
LANES = 128
LEN_ROWS = 16
PRODUCT_VMEM = 50_000_000
DUAL_VMEM = 50_000_000
SMALL_VMEM = 16 << 20
EAST, SOUTH, WEST, NORTH = 0, 1, 2, 3
step_sizes = (0.55, 0.75)
momenta = (0.0, 0.15)


F32 = jnp.float32
BF16 = jnp.bfloat16


def shifted(shard, axis, by):
    peers = lax.axis_size(axis)
    return lax.ppermute(shard, axis, [(i, (i + by) % peers) for i in range(peers)])


def copies_of_all(shard, axis):
    peers = lax.axis_size(axis)
    return lax.all_to_all(
        jnp.broadcast_to(shard[None], (peers, *shard.shape)), axis, 0, 0, tiled=True
    )


def exchanged(outgoing):
    east, west, south, north = outgoing
    return (
        shifted(west, "sy", -1),
        shifted(east, "sy", 1),
        shifted(north, "sx", -1),
        shifted(south, "sx", 1),
    )


def dot(a, b, contract=((1,), (0,))):
    return lax.dot_general(a, b, (contract, ((), ())), preferred_element_type=F32)


def below(limit_rows, rows):
    return lax.broadcasted_iota(jnp.int32, (rows, LANES), 0).astype(F32) < limit_rows


VMEM = pl.BlockSpec(memory_space=pltpu.VMEM)
SMEM = pl.BlockSpec(memory_space=pltpu.SMEM)
HBM = pl.BlockSpec(memory_space=pltpu.HBM)


def loads_of(taut, wrinkle, held, arrived):
    rows = held.shape[2] // 2
    copies = {}
    for sub in range(2):
        for half in range(2):
            at = pl.ds(half * rows, rows)
            copies[sub, half] = [
                pltpu.make_async_copy(
                    source.at[0, sub, at], held.at[sub, which, at], arrived.at[sub, half, which]
                )
                for which, source in enumerate((taut, wrinkle))
            ]
    return copies


def start_loads(copies):
    for pair in copies.values():
        for copy in pair:
            copy.start()


def product(copies, flags, held, vectors, result, outgoing, rows):
    east, west, south, north = outgoing
    for (sub, half), pair in copies.items():
        for copy in pair:
            copy.wait()
        own = vectors[sub]
        at = slice(2 * rows * half, 2 * rows * (half + 1))
        flag = flags[sub].astype(F32)
        value = dot(held[sub, 0, at], own) + flag * dot(held[sub, 1, at], own)
        near, far = value[:rows], value[rows:]
        result[sub, 2 * half] = near
        result[sub, 2 * half + 1] = far
        if half == 0:
            if sub == 1:
                east[0, :rows] = near.astype(BF16)
            south[sub, :rows] = far.astype(BF16)
        else:
            if sub == 0:
                west[0, :rows] = near.astype(BF16)
            north[sub, :rows] = far.astype(BF16)


def product_call(
    body, flags, taut, wrinkle, others, specs, rows, extra_rows, more_out=(), more_scratch=(),
    limit=PRODUCT_VMEM,
):
    order = 4 * rows
    sent = rows + extra_rows
    outs = [
        jax.ShapeDtypeStruct((2, 4, rows, LANES), F32),
        jax.ShapeDtypeStruct((1, sent, LANES), BF16),
        jax.ShapeDtypeStruct((1, sent, LANES), BF16),
        jax.ShapeDtypeStruct((2, sent, LANES), BF16),
        jax.ShapeDtypeStruct((2, sent, LANES), BF16),
        *more_out,
    ]
    return pl.pallas_call(
        body,
        out_shape=outs,
        in_specs=[SMEM, HBM, HBM, *specs],
        out_specs=[VMEM] * len(outs),
        scratch_shapes=[
            pltpu.VMEM((2, order, LANES), BF16),
            pltpu.VMEM((2, 2, order, order), BF16),
            pltpu.SemaphoreType.DMA((2, 2, 2)),
            *more_scratch,
        ],
        compiler_params=pltpu.CompilerParams(vmem_limit_bytes=limit),
    )(flags, taut, wrinkle, *others)


def first_body(flags, taut, wrinkle, sent, from_left, from_up, pieces,
               result, east, west, south, north, lens, vectors, held, arrived):
    rows = sent.shape[2] - LEN_ROWS
    copies = loads_of(taut, wrinkle, held, arrived)
    start_loads(copies)

    def limit(rows_of):
        return rows_of[0:8].astype(F32) * 16.0 + rows_of[8:16].astype(F32)

    for sub in range(2):
        vectors[sub, 0 * rows : 1 * rows] = sent[sub, 0, :rows]
        vectors[sub, 1 * rows : 2 * rows] = sent[sub, 1, :rows]
        vectors[sub, 3 * rows : 4 * rows] = -from_up[sub, :rows]
        lens[sub, 0] = limit(sent[sub, 0, rows:])
        lens[sub, 1] = limit(sent[sub, 1, rows:])
        lens[sub, 3] = limit(from_up[sub, rows:])
        south[sub, rows:] = pieces[sub, SOUTH]
        north[sub, rows:] = pieces[sub, NORTH]
    vectors[0, 2 * rows : 3 * rows] = -from_left[0, :rows]
    vectors[1, 2 * rows : 3 * rows] = -sent[0, 0, :rows]
    lens[0, 2] = limit(from_left[0, rows:])
    lens[1, 2] = limit(sent[0, 0, rows:])
    east[0, rows:] = pieces[1, EAST]
    west[0, rows:] = pieces[0, WEST]
    product(copies, flags, held, vectors, result, (east, west, south, north), rows)


def partner(result, incoming, sub, kind, rows):
    east, west, south, north = incoming
    if kind == EAST:
        return result[1, WEST] if sub == 0 else east[0, :rows].astype(F32)
    if kind == WEST:
        return result[0, EAST] if sub == 1 else west[0, :rows].astype(F32)
    if kind == SOUTH:
        return south[sub, :rows].astype(F32)
    return north[sub, :rows].astype(F32)


def preconditioned_part(result, incoming, lens, sub, kind, rows):
    gap = result[sub, kind] - partner(result, incoming, sub, kind, rows)
    return jnp.where(below(lens[sub, kind, 0:1], rows), 0.5 * gap, 0.0)


def fill_multipliers(number, result, incoming, lens, earlier, kept, vectors):
    rows = result.shape[2]
    for sub in range(2):
        for kind in range(4):
            part = preconditioned_part(result, incoming, lens, sub, kind, rows)
            if number == 0:
                total = step_sizes[0] * part
                if kept is not None:
                    kept[sub, kind] = part
            else:
                before = earlier[sub, kind]
                total = step_sizes[0] * before + step_sizes[1] * (part + momenta[1] * before)
                if kept is not None and kind < 2:
                    kept[sub, kind] = total
            vectors[sub, kind * rows : (kind + 1) * rows] = total.astype(BF16)


def terms_body(number, result, east, west, south, north, lens, coupling, *rest):
    if number == 0:
        terms, vectors = rest
        earlier = None
    else:
        earlier, terms, vectors = rest
    fill_multipliers(number, result, (east, west, south, north), lens, earlier, None, vectors)
    both = vectors[...].reshape(2 * vectors.shape[1], LANES)
    terms[...] = dot(coupling[...], both).astype(BF16)


def terms_call(number, result, incoming, lens, coupling, earlier):
    rows = result.shape[2]
    return pl.pallas_call(
        functools.partial(terms_body, number),
        out_shape=jax.ShapeDtypeStruct((2 * CORNERS, LANES), BF16),
        in_specs=[VMEM] * (7 + len(earlier)),
        out_specs=VMEM,
        scratch_shapes=[pltpu.VMEM((2, 4 * rows, LANES), BF16)],
        compiler_params=pltpu.CompilerParams(vmem_limit_bytes=SMALL_VMEM),
    )(result, *incoming, lens, coupling, *earlier)


def dual_body(number, flags, taut, wrinkle, lens, *rest):
    count = 5 + number
    sources, rest = rest[:count], rest[count:]
    result, east, west, south, north, kept, vectors, held, arrived, *rest = rest
    local_copies, loaded = rest[:count], rest[count]
    rows = result.shape[2]
    moves = [
        pltpu.make_async_copy(source, target, loaded.at[k])
        for k, (source, target) in enumerate(zip(sources, local_copies))
    ]
    for move in moves:
        move.start()
    copies = loads_of(taut, wrinkle, held, arrived)
    start_loads(copies)
    for move in moves:
        move.wait()
    fill_multipliers(
        number, local_copies[0], local_copies[1:5], lens,
        local_copies[5] if number else None, kept, vectors,
    )
    product(copies, flags, held, vectors, result, (east, west, south, north), rows)


def correction_body(terms, select, pieces, east_piece, west_piece, south_piece, north_piece,
                    loads, from_left, from_up, lens, out):
    rows = loads.shape[2]
    segments = pieces.shape[2] // SLOT
    solved = dot(select[...], terms[...]).astype(BF16)
    group = [solved[SLOT * k : SLOT * (k + 1)] for k in range(8)]
    other = {
        (0, EAST): (group[1], pieces[1, WEST]),
        (1, WEST): (group[0], pieces[0, EAST]),
        (0, NORTH): (group[2], north_piece[0, rows:]),
        (1, NORTH): (group[3], north_piece[1, rows:]),
        (0, SOUTH): (group[4], south_piece[0, rows:]),
        (1, SOUTH): (group[5], south_piece[1, rows:]),
        (0, WEST): (group[6], west_piece[0, rows:]),
        (1, EAST): (group[7], east_piece[0, rows:]),
    }
    for sub in range(2):
        for kind in range(4):
            values, piece = other[sub, kind]
            stacked = jnp.concatenate([group[sub], -values], axis=0)
            if kind < 2:
                start = 0.5 * loads[sub, kind]
            elif kind == NORTH:
                start = -from_up[sub, :rows].astype(F32)
            elif sub == 1:
                start = -0.5 * loads[0, EAST]
            else:
                start = -from_left[0, :rows].astype(F32)
            for segment in range(segments):
                low = segment * LANES
                high = min(rows, low + LANES)
                at = slice(segment * SLOT, (segment + 1) * SLOT)
                both = jnp.concatenate([pieces[sub, kind, at], piece[at]], axis=0)
                shift = dot(both, stacked, ((0,), (0,)))[: high - low]
                spot = lax.broadcasted_iota(jnp.int32, (high - low, LANES), 0) + low
                live = spot.astype(F32) < lens[sub, kind, 0:1]
                out[sub, kind, low:high] = start[low:high] - jnp.where(live, 0.5 * shift, 0.0)


def correction_call(*operands):
    rows = operands[7].shape[2]
    return pl.pallas_call(
        correction_body,
        out_shape=jax.ShapeDtypeStruct((2, 4, rows, LANES), F32),
        in_specs=[VMEM] * len(operands),
        out_specs=VMEM,
        compiler_params=pltpu.CompilerParams(vmem_limit_bytes=SMALL_VMEM),
    )(*operands)


def residual_body(flags, taut, wrinkle, earlier, from_east, from_west, from_south, from_north,
                  lens, base, result, east, west, south, north, vectors, held, arrived):
    rows = earlier.shape[2]
    incoming = (from_east, from_west, from_south, from_north)
    copies = loads_of(taut, wrinkle, held, arrived)
    start_loads(copies)
    for sub in range(2):
        for kind in range(4):
            gap = preconditioned_part(earlier, incoming, lens, sub, kind, rows)
            vectors[sub, kind * rows : (kind + 1) * rows] = (base[sub, kind] - gap).astype(BF16)
    product(copies, flags, held, vectors, result, (east, west, south, north), rows)


def last_body(result, east, south, lens, out):
    rows = result.shape[2]
    for sub in range(2):
        for kind in range(2):
            out[sub, kind] = preconditioned_part(
                result, (east, None, south, None), lens, sub, kind, rows
            )


def coarse_rows(coarse_inverse, corner_map):
    row_count, col_count = coarse_inverse.shape
    rows_of = lax.axis_size("sx")
    cols_of = lax.axis_size("sy")
    per = 2 * CORNERS
    row_index = lax.axis_index("sx")
    row_maps = copies_of_all(corner_map.reshape(1, per), "sy").reshape(cols_of * per)
    codes = jnp.concatenate([row_maps // 32, row_maps % 32]).astype(BF16)
    code_rows = codes.shape[0] // LANES
    tile = jnp.pad(coarse_inverse, ((0, 0), (0, LANES - col_count)))
    message = jnp.concatenate([tile, codes.reshape(code_rows, LANES)], axis=0)
    message = jnp.pad(message, ((0, 64 - message.shape[0]), (0, 0)))
    arrived = copies_of_all(message, "sx")
    columns = arrived[:, :row_count].reshape(rows_of * row_count, LANES)
    codes = arrived[:, row_count : row_count + code_rows].astype(jnp.int32)
    codes = codes.reshape(rows_of, 2, cols_of, per)
    maps = codes[:, 0] * 32 + codes[:, 1]
    at = lambda by: lax.dynamic_index_in_dim(maps, (row_index + by) % rows_of, 0, False)
    here, up, down = at(0), at(-1 + rows_of), at(1)
    groups = [
        here[:, :CORNERS],
        here[:, CORNERS:],
        up[:, :CORNERS],
        up[:, CORNERS:],
        down[:, :CORNERS],
        down[:, CORNERS:],
        jnp.roll(here, 1, axis=0)[:, CORNERS:],
        jnp.roll(here, -1, axis=0)[:, :CORNERS],
    ]
    wanted = jnp.pad(
        jnp.stack(groups, axis=1), ((0, 0), (0, 0), (0, SLOT - CORNERS)), constant_values=-1
    ).reshape(-1, 1)
    coarse_order = rows_of * row_count
    pick = (wanted == jnp.arange(coarse_order)[None]).astype(BF16)
    chosen = dot(pick, columns).astype(BF16).reshape(cols_of, -1, LANES)
    chosen = lax.all_to_all(chosen, "sy", 0, 0, tiled=True)
    flat = maps.reshape(-1)
    spot = (flat // col_count) * LANES + flat % col_count
    place = (jnp.arange(cols_of * LANES)[:, None] == spot[None]).astype(BF16)
    chosen = jnp.moveaxis(chosen, 0, 1).reshape(chosen.shape[1], -1)
    return dot(chosen, place).astype(BF16)


def local(
    adjoint_loads,
    dual_taut,
    dual_wrinkle,
    dirichlet_taut,
    dirichlet_wrinkle,
    coupling,
    coarse_inverse,
    wrinkled,
    edge_lengths,
    corner_map,
):
    rows = adjoint_loads.shape[3]
    order = 4 * rows
    loads = adjoint_loads[0]
    flags = wrinkled[0]
    columns = lax.axis_index("sy") * 2 + jnp.arange(2)
    exists = jnp.stack(
        [
            columns < 2 * lax.axis_size("sy") - 1,
            jnp.broadcast_to(lax.axis_index("sx") < lax.axis_size("sx") - 1, (2,)),
        ],
        axis=1,
    )
    own_lens = jnp.where(exists, edge_lengths[0], 0)[:, :, None, None]
    position = lax.broadcasted_iota(jnp.int32, (2, 2, rows, LANES), 2)
    loads = jnp.where(position < own_lens, loads, 0.0)
    digits = jnp.where(
        lax.broadcasted_iota(jnp.int32, (2, 2, LEN_ROWS, LANES), 2) < LEN_ROWS // 2,
        own_lens // 16,
        own_lens % 16,
    )
    sent = jnp.concatenate([(0.5 * loads).astype(BF16), digits.astype(BF16)], axis=2)
    from_left = shifted(sent[1:, 0], "sy", 1)
    from_up = shifted(sent[:, 1], "sx", 1)

    segments = -(-rows // LANES)
    pieces = coupling[0].reshape(2, CORNERS, 4, rows)
    pieces = jnp.pad(
        pieces, ((0, 0), (0, SLOT - CORNERS), (0, 0), (0, segments * LANES - rows))
    )
    pieces = pieces.reshape(2, SLOT, 4, segments, LANES)
    pieces = jnp.transpose(pieces, (0, 2, 3, 1, 4)).reshape(2, 4, segments * SLOT, LANES)
    blank = jnp.zeros((CORNERS, order), BF16)
    wide = jnp.concatenate(
        [
            jnp.concatenate([coupling[0, 0], blank], axis=1),
            jnp.concatenate([blank, coupling[0, 1]], axis=1),
        ],
        axis=0,
    )
    select = coarse_rows(coarse_inverse, corner_map)

    result, *outgoing, lens = product_call(
        first_body, flags, dirichlet_taut, dirichlet_wrinkle,
        (sent, from_left, from_up, pieces), [VMEM] * 4, rows, segments * SLOT,
        (jax.ShapeDtypeStruct((2, 4, 8, LANES), F32),),
    )
    incoming = exchanged(outgoing)
    neighbour_pieces = incoming
    kept = None
    for number in range(2):
        earlier = () if number == 0 else (kept,)
        terms = terms_call(number, result, incoming, lens, wide, earlier)
        everyone = copies_of_all(terms, ("sx", "sy")).reshape(-1, LANES)
        sources = (result, *incoming, *earlier)
        result, *outgoing, kept = product_call(
            functools.partial(dual_body, number), flags, dual_taut, dual_wrinkle,
            (lens, *sources), [VMEM] + [HBM] * len(sources), rows, 0,
            (jax.ShapeDtypeStruct((2, 4 - 2 * number, rows, LANES), F32),),
            [
                *[pltpu.VMEM(x.shape, x.dtype) for x in sources],
                pltpu.SemaphoreType.DMA((len(sources),)),
            ],
            DUAL_VMEM,
        )
        incoming = exchanged(outgoing)
        base = correction_call(
            everyone, select, pieces, *neighbour_pieces, loads, from_left, from_up, lens
        )
        result, *outgoing = product_call(
            residual_body, flags, dirichlet_taut, dirichlet_wrinkle,
            (result, *incoming, lens, base), [VMEM] * 7, rows, 0,
        )
        if number == 0:
            incoming = exchanged(outgoing)
    _, west, _, north = outgoing
    preconditioned = pl.pallas_call(
        last_body,
        out_shape=jax.ShapeDtypeStruct((2, 2, rows, LANES), F32),
        in_specs=[VMEM] * 4,
        out_specs=VMEM,
        compiler_params=pltpu.CompilerParams(vmem_limit_bytes=SMALL_VMEM),
    )(result, shifted(west, "sy", -1), shifted(north, "sx", -1), lens)
    return kept[None], preconditioned[None]


def solution(mesh):
    placed = (
        P("sx", "sy", None, None, None),
        P("sx", "sy", None, None),
        P("sx", "sy", None, None),
        P("sx", "sy", None, None),
        P("sx", "sy", None, None),
        P("sx", "sy", None, None),
        P("sx", "sy"),
        P("sx", "sy"),
        P("sx", "sy", None),
        P("sx", "sy", None),
    )
    return jax.shard_map(
        local,
        mesh=mesh,
        in_specs=placed,
        out_specs=(P("sx", "sy", None, None, None), P("sx", "sy", None, None, None)),
        check_vma=False,
    )
```

```python
import functools

import jax
import jax.numpy as jnp
from jax import lax
from jax.experimental import pallas as pl
from jax.experimental.pallas import tpu as pltpu
from jax.sharding import PartitionSpec as P


CORNERS = 12
SLOT = 16
LANES = 128
LEN_ROWS = 16
PRODUCT_VMEM = 50_000_000
SMALL_VMEM = 16 << 20
EAST, SOUTH, WEST, NORTH = 0, 1, 2, 3
step_sizes = (0.55, 0.75)
momenta = (0.0, 0.15)


F32 = jnp.float32
BF16 = jnp.bfloat16


def shifted(shard, axis, by):
    peers = lax.axis_size(axis)
    return lax.ppermute(shard, axis, [(i, (i + by) % peers) for i in range(peers)])


def copies_of_all(shard, axis):
    peers = lax.axis_size(axis)
    return lax.all_to_all(
        jnp.broadcast_to(shard[None], (peers, *shard.shape)), axis, 0, 0, tiled=True
    )


def exchanged(outgoing):
    east, west, south, north = outgoing
    from_east = None if west is None else shifted(west, "sy", -1)
    from_west = None if east is None else shifted(east, "sy", 1)
    from_south = None if north is None else shifted(north, "sx", -1)
    from_north = None if south is None else shifted(south, "sx", 1)
    return from_east, from_west, from_south, from_north


def dot(a, b, contract=((1,), (0,))):
    return lax.dot_general(a, b, (contract, ((), ())), preferred_element_type=F32)


def below(limit_rows, rows):
    return lax.broadcasted_iota(jnp.int32, (rows, LANES), 0).astype(F32) < limit_rows


VMEM = pl.BlockSpec(memory_space=pltpu.VMEM)
SMEM = pl.BlockSpec(memory_space=pltpu.SMEM)
HBM = pl.BlockSpec(memory_space=pltpu.HBM)


def loads_of(taut, wrinkle, held, arrived):
    rows = held.shape[2] // 2
    copies = {}
    for sub in range(2):
        for half in range(2):
            at = pl.ds(half * rows, rows)
            copies[sub, half] = [
                pltpu.make_async_copy(
                    source.at[0, sub, at], held.at[sub, which, at], arrived.at[sub, half, which]
                )
                for which, source in enumerate((taut, wrinkle))
            ]
    return copies


def start_loads(copies):
    for pair in copies.values():
        for copy in pair:
            copy.start()


def product(copies, flags, held, vectors, result, outgoing, rows):
    east, west, south, north = outgoing
    for (sub, half), pair in copies.items():
        for copy in pair:
            copy.wait()
        own = vectors[sub]
        at = slice(2 * rows * half, 2 * rows * (half + 1))
        flag = flags[sub].astype(F32)
        value = dot(held[sub, 0, at], own) + flag * dot(held[sub, 1, at], own)
        near, far = value[:rows], value[rows:]
        result[sub, 2 * half] = near
        result[sub, 2 * half + 1] = far
        if half == 0:
            if sub == 1:
                east[0, :rows] = near.astype(BF16)
            south[sub, :rows] = far.astype(BF16)
        else:
            if sub == 0:
                west[0, :rows] = near.astype(BF16)
            north[sub, :rows] = far.astype(BF16)


def product_call(
    body, flags, taut, wrinkle, others, specs, rows, extra_rows, more_out=(), more_scratch=(),
    limit=PRODUCT_VMEM,
):
    order = 4 * rows
    sent = rows + extra_rows
    outs = [
        jax.ShapeDtypeStruct((2, 4, rows, LANES), F32),
        jax.ShapeDtypeStruct((1, sent, LANES), BF16),
        jax.ShapeDtypeStruct((1, sent, LANES), BF16),
        jax.ShapeDtypeStruct((2, sent, LANES), BF16),
        jax.ShapeDtypeStruct((2, sent, LANES), BF16),
        *more_out,
    ]
    return pl.pallas_call(
        body,
        out_shape=outs,
        in_specs=[SMEM, HBM, HBM, *specs],
        out_specs=[VMEM] * len(outs),
        scratch_shapes=[
            pltpu.VMEM((2, order, LANES), BF16),
            pltpu.VMEM((2, 2, order, order), BF16),
            pltpu.SemaphoreType.DMA((2, 2, 2)),
            *more_scratch,
        ],
        compiler_params=pltpu.CompilerParams(vmem_limit_bytes=limit),
    )(flags, taut, wrinkle, *others)


def live_length(spots, lengths, sub, kind, last):
    exists = 2 * spots[1] + sub < last[0] if kind == EAST else spots[0] < last[1]
    return jnp.where(exists, lengths[sub, kind], 0)


def pack_body(last, spots, lengths, loads, east, south):
    rows = loads.shape[2]
    for target, slot, sub, kind in (
        (east, 0, 1, EAST), (south, 0, 0, SOUTH), (south, 1, 1, SOUTH)
    ):
        length = live_length(spots, lengths, sub, kind, last)
        live = lax.broadcasted_iota(jnp.int32, (rows, LANES), 0) < length
        target[slot, :rows] = jnp.where(live, 0.5 * loads[sub, kind], 0.0).astype(BF16)
        upper = lax.broadcasted_iota(jnp.int32, (LEN_ROWS, LANES), 0) < LEN_ROWS // 2
        digits = jnp.where(upper, length >> 4, length & 15)
        target[slot, rows:] = digits.astype(F32).astype(BF16)


def first_body(last, flags, taut, wrinkle, spots, lengths, loads, from_left, from_up, pieces,
               result, east, west, south, north, lens, start, vectors, held, arrived):
    rows = loads.shape[2]
    copies = loads_of(taut, wrinkle, held, arrived)
    start_loads(copies)

    def limit(rows_of):
        return rows_of[0:8].astype(F32) * 16.0 + rows_of[8:16].astype(F32)

    for sub in range(2):
        for kind in (EAST, SOUTH):
            length = live_length(spots, lengths, sub, kind, last)
            live = lax.broadcasted_iota(jnp.int32, (rows, LANES), 0) < length
            start[sub, kind] = jnp.where(live, 0.5 * loads[sub, kind], 0.0)
            lens[sub, kind] = jnp.broadcast_to(length, (8, LANES)).astype(F32)
        start[sub, NORTH] = -from_up[sub, :rows].astype(F32)
        lens[sub, NORTH] = limit(from_up[sub, rows:])
        south[sub, rows:] = pieces[sub, SOUTH]
        north[sub, rows:] = pieces[sub, NORTH]
    start[0, WEST] = -from_left[0, :rows].astype(F32)
    start[1, WEST] = -start[0, EAST]
    lens[0, WEST] = limit(from_left[0, rows:])
    lens[1, WEST] = lens[0, EAST]
    east[0, rows:] = pieces[1, EAST]
    west[0, rows:] = pieces[0, WEST]
    for sub in range(2):
        for kind in range(4):
            vectors[sub, kind * rows : (kind + 1) * rows] = start[sub, kind].astype(BF16)
    product(copies, flags, held, vectors, result, (east, west, south, north), rows)


def partner(result, incoming, sub, kind, rows):
    east, west, south, north = incoming
    if kind == EAST:
        return result[1, WEST] if sub == 0 else east[0, :rows].astype(F32)
    if kind == WEST:
        return result[0, EAST] if sub == 1 else west[0, :rows].astype(F32)
    if kind == SOUTH:
        return south[sub, :rows].astype(F32)
    return north[sub, :rows].astype(F32)


def preconditioned_part(result, incoming, lens, sub, kind, rows):
    gap = result[sub, kind] - partner(result, incoming, sub, kind, rows)
    return jnp.where(below(lens[sub, kind, 0:1], rows), 0.5 * gap, 0.0)


def fill_multipliers(number, result, incoming, lens, earlier, kept, vectors):
    rows = result.shape[2]
    for sub in range(2):
        for kind in range(4):
            part = preconditioned_part(result, incoming, lens, sub, kind, rows)
            if number == 0:
                total = step_sizes[0] * part
                if kept is not None:
                    kept[sub, kind] = part
            else:
                before = earlier[sub, kind]
                total = step_sizes[0] * before + step_sizes[1] * (part + momenta[1] * before)
                if kept is not None and kind < 2:
                    kept[sub, kind] = total
            vectors[sub, kind * rows : (kind + 1) * rows] = total.astype(BF16)


def coarse_terms(coupling, vectors, terms, stacked):
    for sub in range(2):
        stacked[sub * CORNERS : (sub + 1) * CORNERS] = dot(coupling[0, sub], vectors[sub])
    terms[...] = stacked[...].astype(BF16)


def first_terms_body(result, east, west, south, north, lens, coupling, pieces,
                     terms, vectors, kept, paired, stacked):
    rows = result.shape[2]
    fill_multipliers(0, result, (east, west, south, north), lens, None, kept, vectors)
    coarse_terms(coupling, vectors, terms, stacked)
    other = {
        (0, EAST): pieces[1, WEST],
        (1, WEST): pieces[0, EAST],
        (0, NORTH): north[0, rows:],
        (1, NORTH): north[1, rows:],
        (0, SOUTH): south[0, rows:],
        (1, SOUTH): south[1, rows:],
        (0, WEST): west[0, rows:],
        (1, EAST): east[0, rows:],
    }
    for (sub, kind), piece in other.items():
        for segment in range(pieces.shape[2] // SLOT):
            at = slice(segment * SLOT, (segment + 1) * SLOT)
            low = 2 * segment * SLOT
            paired[sub, kind, low : low + SLOT] = pieces[sub, kind, at]
            paired[sub, kind, low + SLOT : low + 2 * SLOT] = piece[at]


def second_terms_body(result, east, west, south, north, lens, coupling, earlier,
                      terms, vectors, kept, stacked):
    fill_multipliers(1, result, (east, west, south, north), lens, earlier, kept, vectors)
    coarse_terms(coupling, vectors, terms, stacked)


def terms_call(number, result, incoming, lens, coupling, extra):
    rows = result.shape[2]
    outs = [
        jax.ShapeDtypeStruct((2 * CORNERS, LANES), BF16),
        jax.ShapeDtypeStruct((2, 4 * rows, LANES), BF16),
        jax.ShapeDtypeStruct((2, 4 - 2 * number, rows, LANES), F32),
    ]
    if number == 0:
        outs.append(jax.ShapeDtypeStruct((2, 4, 2 * extra.shape[2], LANES), BF16))
    return pl.pallas_call(
        second_terms_body if number else first_terms_body,
        out_shape=outs,
        in_specs=[VMEM] * 8,
        out_specs=[VMEM] * len(outs),
        scratch_shapes=[pltpu.VMEM((2 * CORNERS, LANES), F32)],
        compiler_params=pltpu.CompilerParams(vmem_limit_bytes=SMALL_VMEM),
    )(result, *incoming, lens, coupling, extra)


def dual_body(flags, taut, wrinkle, source, result, east, west, south, north,
              vectors, held, arrived, loaded):
    rows = result.shape[2]
    own = pltpu.make_async_copy(source, vectors, loaded)
    own.start()
    copies = loads_of(taut, wrinkle, held, arrived)
    start_loads(copies)
    own.wait()
    product(copies, flags, held, vectors, result, (east, west, south, north), rows)


def correction_body(terms, select, paired, start, lens, out):
    rows = start.shape[2]
    solved = dot(select[...], terms[...]).astype(BF16)
    group = [solved[SLOT * k : SLOT * (k + 1)] for k in range(8)]
    other = {
        (0, EAST): group[1],
        (1, WEST): group[0],
        (0, NORTH): group[2],
        (1, NORTH): group[3],
        (0, SOUTH): group[4],
        (1, SOUTH): group[5],
        (0, WEST): group[6],
        (1, EAST): group[7],
    }
    for (sub, kind), values in other.items():
        stacked = jnp.concatenate([group[sub], -values], axis=0)
        for segment in range(paired.shape[2] // (2 * SLOT)):
            low = segment * LANES
            high = min(rows, low + LANES)
            both = paired[sub, kind, 2 * segment * SLOT : 2 * (segment + 1) * SLOT]
            shift = dot(both, stacked, ((0,), (0,)))[: high - low]
            spot = lax.broadcasted_iota(jnp.int32, (high - low, LANES), 0) + low
            live = spot.astype(F32) < lens[sub, kind, 0:1]
            out[sub, kind, low:high] = start[sub, kind, low:high] - jnp.where(
                live, 0.5 * shift, 0.0
            )


def correction_call(*operands):
    rows = operands[3].shape[2]
    return pl.pallas_call(
        correction_body,
        out_shape=jax.ShapeDtypeStruct((2, 4, rows, LANES), F32),
        in_specs=[VMEM] * len(operands),
        out_specs=VMEM,
        compiler_params=pltpu.CompilerParams(vmem_limit_bytes=SMALL_VMEM),
    )(*operands)


def residual_body(flags, taut, wrinkle, earlier, from_east, from_west, from_south, from_north,
                  lens, base, result, east, west, south, north, vectors, held, arrived):
    rows = earlier.shape[2]
    incoming = (from_east, from_west, from_south, from_north)
    copies = loads_of(taut, wrinkle, held, arrived)
    start_loads(copies)
    for sub in range(2):
        for kind in range(4):
            gap = preconditioned_part(earlier, incoming, lens, sub, kind, rows)
            vectors[sub, kind * rows : (kind + 1) * rows] = (base[sub, kind] - gap).astype(BF16)
    product(copies, flags, held, vectors, result, (east, west, south, north), rows)


def last_body(result, east, south, lens, out):
    rows = result.shape[2]
    for sub in range(2):
        for kind in range(2):
            out[sub, kind] = preconditioned_part(
                result, (east, None, south, None), lens, sub, kind, rows
            )


def coarse_rows(coarse_inverse, corner_map):
    row_count, col_count = coarse_inverse.shape
    rows_of = lax.axis_size("sx")
    cols_of = lax.axis_size("sy")
    per = 2 * CORNERS
    row_index = lax.axis_index("sx")
    row_maps = copies_of_all(corner_map.reshape(1, per), "sy").reshape(cols_of * per)
    codes = jnp.concatenate([row_maps // 32, row_maps % 32]).astype(BF16)
    code_rows = codes.shape[0] // LANES
    tile = jnp.pad(coarse_inverse, ((0, 0), (0, LANES - col_count)))
    message = jnp.concatenate([tile, codes.reshape(code_rows, LANES)], axis=0)
    message = jnp.pad(message, ((0, 64 - message.shape[0]), (0, 0)))
    arrived = copies_of_all(message, "sx")
    columns = arrived[:, :row_count].reshape(rows_of * row_count, LANES)
    codes = arrived[:, row_count : row_count + code_rows].astype(jnp.int32)
    codes = codes.reshape(rows_of, 2, cols_of, per)
    maps = codes[:, 0] * 32 + codes[:, 1]
    at = lambda by: lax.dynamic_index_in_dim(maps, (row_index + by) % rows_of, 0, False)
    here, up, down = at(0), at(-1 + rows_of), at(1)
    groups = [
        here[:, :CORNERS],
        here[:, CORNERS:],
        up[:, :CORNERS],
        up[:, CORNERS:],
        down[:, :CORNERS],
        down[:, CORNERS:],
        jnp.roll(here, 1, axis=0)[:, CORNERS:],
        jnp.roll(here, -1, axis=0)[:, :CORNERS],
    ]
    wanted = jnp.pad(
        jnp.stack(groups, axis=1), ((0, 0), (0, 0), (0, SLOT - CORNERS)), constant_values=-1
    ).reshape(-1, 1)
    coarse_order = rows_of * row_count
    pick = (wanted == jnp.arange(coarse_order)[None]).astype(BF16)
    chosen = dot(pick, columns).astype(BF16).reshape(cols_of, -1, LANES)
    chosen = lax.all_to_all(chosen, "sy", 0, 0, tiled=True)
    flat = maps.reshape(-1)
    spot = (flat // col_count) * LANES + flat % col_count
    place = (jnp.arange(cols_of * LANES)[:, None] == spot[None]).astype(BF16)
    chosen = jnp.moveaxis(chosen, 0, 1).reshape(chosen.shape[1], -1)
    return dot(chosen, place).astype(BF16)


def steps(
    adjoint_loads,
    dual_taut,
    dual_wrinkle,
    dirichlet_taut,
    dirichlet_wrinkle,
    coupling,
    coarse_inverse,
    wrinkled,
    edge_lengths,
    corner_map,
):
    rows = adjoint_loads.shape[3]
    loads = adjoint_loads[0]
    flags = wrinkled[0]
    lengths = edge_lengths[0]
    spots = jnp.stack([lax.axis_index("sx"), lax.axis_index("sy")]).astype(jnp.int32)
    last = (2 * lax.axis_size("sy") - 1, lax.axis_size("sx") - 1)
    east, south = pl.pallas_call(
        functools.partial(pack_body, last),
        out_shape=[
            jax.ShapeDtypeStruct((1, rows + LEN_ROWS, LANES), BF16),
            jax.ShapeDtypeStruct((2, rows + LEN_ROWS, LANES), BF16),
        ],
        in_specs=[SMEM, SMEM, VMEM],
        out_specs=[VMEM] * 2,
        compiler_params=pltpu.CompilerParams(vmem_limit_bytes=SMALL_VMEM),
    )(spots, lengths, loads)
    _, from_left, _, from_up = exchanged((east, None, south, None))

    segments = -(-rows // LANES)
    pieces = coupling[0].reshape(2, CORNERS, 4, rows)
    pieces = jnp.pad(
        pieces, ((0, 0), (0, SLOT - CORNERS), (0, 0), (0, segments * LANES - rows))
    )
    pieces = pieces.reshape(2, SLOT, 4, segments, LANES)
    pieces = jnp.transpose(pieces, (0, 2, 3, 1, 4)).reshape(2, 4, segments * SLOT, LANES)
    select = coarse_rows(coarse_inverse, corner_map)

    result, *outgoing, lens, start = product_call(
        functools.partial(first_body, last), flags, dirichlet_taut, dirichlet_wrinkle,
        (spots, lengths, loads, from_left, from_up, pieces), [SMEM] * 2 + [VMEM] * 4,
        rows, segments * SLOT,
        (
            jax.ShapeDtypeStruct((2, 4, 8, LANES), F32),
            jax.ShapeDtypeStruct((2, 4, rows, LANES), F32),
        ),
    )
    for number in range(2):
        incoming = exchanged(outgoing)
        if number == 0:
            terms, vectors, kept, paired = terms_call(
                0, result, incoming, lens, coupling, pieces
            )
        else:
            terms, vectors, kept = terms_call(1, result, incoming, lens, coupling, kept)
        everyone = copies_of_all(terms, ("sx", "sy")).reshape(-1, LANES)
        result, *outgoing = product_call(
            dual_body, flags, dual_taut, dual_wrinkle, (vectors,), [HBM],
            rows, 0, (), [pltpu.SemaphoreType.DMA],
        )
        incoming = exchanged(outgoing)
        base = correction_call(everyone, select, paired, start, lens)
        result, *outgoing = product_call(
            residual_body, flags, dirichlet_taut, dirichlet_wrinkle,
            (result, *incoming, lens, base), [VMEM] * 7, rows, 0,
        )
    _, west, _, north = outgoing
    from_east, _, from_south, _ = exchanged((None, west, None, north))
    preconditioned = pl.pallas_call(
        last_body,
        out_shape=jax.ShapeDtypeStruct((2, 2, rows, LANES), F32),
        in_specs=[VMEM] * 4,
        out_specs=VMEM,
        compiler_params=pltpu.CompilerParams(vmem_limit_bytes=SMALL_VMEM),
    )(result, from_east, from_south, lens)
    return kept[None], preconditioned[None]


def solution(mesh):
    placed = (
        P("sx", "sy", None, None, None),
        P("sx", "sy", None, None),
        P("sx", "sy", None, None),
        P("sx", "sy", None, None),
        P("sx", "sy", None, None),
        P("sx", "sy", None, None),
        P("sx", "sy"),
        P("sx", "sy"),
        P("sx", "sy", None),
        P("sx", "sy", None),
    )
    return jax.shard_map(
        steps,
        mesh=mesh,
        in_specs=placed,
        out_specs=(P("sx", "sy", None, None, None), P("sx", "sy", None, None, None)),
        check_vma=False,
    )
```

```python
import functools

import jax
import jax.numpy as jnp
from jax import lax
from jax.experimental import pallas as pl
from jax.experimental.pallas import tpu as pltpu
from jax.sharding import PartitionSpec as P


CORNERS = 12
SLOT = 16
LANES = 128
LEN_ROWS = 16
PRODUCT_VMEM = 50_000_000
SMALL_VMEM = 16 << 20
EAST, SOUTH, WEST, NORTH = 0, 1, 2, 3
step_sizes = (0.55, 0.75)
momenta = (0.0, 0.15)


F32 = jnp.float32
BF16 = jnp.bfloat16


def shifted(shard, axis, by):
    peers = lax.axis_size(axis)
    return lax.ppermute(shard, axis, [(i, (i + by) % peers) for i in range(peers)])


def copies_of_all(shard, axis):
    peers = lax.axis_size(axis)
    return lax.all_to_all(
        jnp.broadcast_to(shard[None], (peers, *shard.shape)), axis, 0, 0, tiled=True
    )


def exchanged(outgoing):
    east, west, south, north = outgoing
    from_east = None if west is None else shifted(west, "sy", -1)
    from_west = None if east is None else shifted(east, "sy", 1)
    from_south = None if north is None else shifted(north, "sx", -1)
    from_north = None if south is None else shifted(south, "sx", 1)
    return from_east, from_west, from_south, from_north


def dot(a, b, contract=((1,), (0,))):
    return lax.dot_general(a, b, (contract, ((), ())), preferred_element_type=F32)


def below(limit_rows, rows):
    return lax.broadcasted_iota(jnp.int32, (rows, LANES), 0).astype(F32) < limit_rows


VMEM = pl.BlockSpec(memory_space=pltpu.VMEM)
SMEM = pl.BlockSpec(memory_space=pltpu.SMEM)
HBM = pl.BlockSpec(memory_space=pltpu.HBM)


def loads_of(taut, wrinkle, held, arrived):
    rows = held.shape[2] // 2
    copies = {}
    for sub in range(2):
        for half in range(2):
            at = pl.ds(half * rows, rows)
            copies[sub, half] = [
                pltpu.make_async_copy(
                    source.at[0, sub, at], held.at[sub, which, at], arrived.at[sub, half, which]
                )
                for which, source in enumerate((taut, wrinkle))
            ]
    return copies


def start_loads(copies):
    for pair in copies.values():
        for copy in pair:
            copy.start()


def product(copies, flags, held, vectors, result, outgoing, rows):
    east, west, south, north = outgoing
    for (sub, half), pair in copies.items():
        for copy in pair:
            copy.wait()
        own = vectors[sub]
        at = slice(2 * rows * half, 2 * rows * (half + 1))
        flag = flags[sub].astype(F32)
        value = dot(held[sub, 0, at], own) + flag * dot(held[sub, 1, at], own)
        near, far = value[:rows], value[rows:]
        result[sub, 2 * half] = near
        result[sub, 2 * half + 1] = far
        if half == 0:
            if sub == 1:
                east[0, :rows] = near.astype(BF16)
            south[sub, :rows] = far.astype(BF16)
        else:
            if sub == 0:
                west[0, :rows] = near.astype(BF16)
            north[sub, :rows] = far.astype(BF16)


def product_call(
    body, flags, taut, wrinkle, others, specs, rows, extra_rows, more_out=(), limit=PRODUCT_VMEM
):
    order = 4 * rows
    sent = rows + extra_rows
    outs = [
        jax.ShapeDtypeStruct((2, 4, rows, LANES), F32),
        jax.ShapeDtypeStruct((1, sent, LANES), BF16),
        jax.ShapeDtypeStruct((1, sent, LANES), BF16),
        jax.ShapeDtypeStruct((2, sent, LANES), BF16),
        jax.ShapeDtypeStruct((2, sent, LANES), BF16),
        *more_out,
    ]
    return pl.pallas_call(
        body,
        out_shape=outs,
        in_specs=[SMEM, HBM, HBM, *specs],
        out_specs=[VMEM] * len(outs),
        scratch_shapes=[
pltpu.VMEM((2, order, LANES), BF16),
pltpu.VMEM((2, 2, order, order), BF16),
pltpu.SemaphoreType.DMA((2, 2, 2)),
        ],
        compiler_params=pltpu.CompilerParams(vmem_limit_bytes=limit),
    )(flags, taut, wrinkle, *others)


def live_length(spots, lengths, sub, kind, last):
    exists = 2 * spots[1] + sub < last[0] if kind == EAST else spots[0] < last[1]
    return jnp.where(exists, lengths[sub, kind], 0)


def pack_body(last, spots, lengths, loads, east, south):
    rows = loads.shape[2]
    for target, slot, sub, kind in (
        (east, 0, 1, EAST), (south, 0, 0, SOUTH), (south, 1, 1, SOUTH)
    ):
        length = live_length(spots, lengths, sub, kind, last)
        live = lax.broadcasted_iota(jnp.int32, (rows, LANES), 0) < length
        target[slot, :rows] = jnp.where(live, 0.5 * loads[sub, kind], 0.0).astype(BF16)
        upper = lax.broadcasted_iota(jnp.int32, (LEN_ROWS, LANES), 0) < LEN_ROWS // 2
        digits = jnp.where(upper, length >> 4, length & 15)
        target[slot, rows:] = digits.astype(F32).astype(BF16)


def first_body(last, flags, taut, wrinkle, spots, lengths, loads, from_left, from_up, pieces,
               result, east, west, south, north, lens, start, vectors, held, arrived):
    rows = loads.shape[2]
    copies = loads_of(taut, wrinkle, held, arrived)
    start_loads(copies)

    def limit(rows_of):
        return rows_of[0:8].astype(F32) * 16.0 + rows_of[8:16].astype(F32)

    for sub in range(2):
        for kind in (EAST, SOUTH):
            length = live_length(spots, lengths, sub, kind, last)
            live = lax.broadcasted_iota(jnp.int32, (rows, LANES), 0) < length
            start[sub, kind] = jnp.where(live, 0.5 * loads[sub, kind], 0.0)
            lens[sub, kind] = jnp.broadcast_to(length, (8, LANES)).astype(F32)
        start[sub, NORTH] = -from_up[sub, :rows].astype(F32)
        lens[sub, NORTH] = limit(from_up[sub, rows:])
        south[sub, rows:] = pieces[sub, SOUTH]
        north[sub, rows:] = pieces[sub, NORTH]
    start[0, WEST] = -from_left[0, :rows].astype(F32)
    start[1, WEST] = -start[0, EAST]
    lens[0, WEST] = limit(from_left[0, rows:])
    lens[1, WEST] = lens[0, EAST]
    east[0, rows:] = pieces[1, EAST]
    west[0, rows:] = pieces[0, WEST]
    for sub in range(2):
        for kind in range(4):
            vectors[sub, kind * rows : (kind + 1) * rows] = start[sub, kind].astype(BF16)
    product(copies, flags, held, vectors, result, (east, west, south, north), rows)


def partner(result, incoming, sub, kind, rows):
    east, west, south, north = incoming
    if kind == EAST:
        return result[1, WEST] if sub == 0 else east[0, :rows].astype(F32)
    if kind == WEST:
        return result[0, EAST] if sub == 1 else west[0, :rows].astype(F32)
    if kind == SOUTH:
        return south[sub, :rows].astype(F32)
    return north[sub, :rows].astype(F32)


def preconditioned_part(result, incoming, lens, sub, kind, rows):
    gap = result[sub, kind] - partner(result, incoming, sub, kind, rows)
    return jnp.where(below(lens[sub, kind, 0:1], rows), 0.5 * gap, 0.0)


def fill_multipliers(number, result, incoming, lens, earlier, kept, vectors):
    rows = result.shape[2]
    for sub in range(2):
        for kind in range(4):
            part = preconditioned_part(result, incoming, lens, sub, kind, rows)
            if number == 0:
                total = step_sizes[0] * part
                if kept is not None:
                    kept[sub, kind] = part
            else:
                before = earlier[sub, kind]
                total = step_sizes[0] * before + step_sizes[1] * (part + momenta[1] * before)
                if kept is not None and kind < 2:
                    kept[sub, kind] = total
            vectors[sub, kind * rows : (kind + 1) * rows] = total.astype(BF16)


def coarse_terms(coupling, vectors, terms, stacked):
    for sub in range(2):
        stacked[sub * CORNERS : (sub + 1) * CORNERS] = dot(coupling[0, sub], vectors[sub])
    terms[...] = stacked[...].astype(BF16)


def first_terms_body(result, east, west, south, north, lens, coupling, pieces,
                     terms, vectors, kept, paired, stacked):
    rows = result.shape[2]
    fill_multipliers(0, result, (east, west, south, north), lens, None, kept, vectors)
    coarse_terms(coupling, vectors, terms, stacked)
    other = {
        (0, EAST): pieces[1, WEST],
        (1, WEST): pieces[0, EAST],
        (0, NORTH): north[0, rows:],
        (1, NORTH): north[1, rows:],
        (0, SOUTH): south[0, rows:],
        (1, SOUTH): south[1, rows:],
        (0, WEST): west[0, rows:],
        (1, EAST): east[0, rows:],
    }
    for (sub, kind), piece in other.items():
        for segment in range(pieces.shape[2] // SLOT):
            at = slice(segment * SLOT, (segment + 1) * SLOT)
            low = 2 * segment * SLOT
            paired[sub, kind, low : low + SLOT] = pieces[sub, kind, at]
            paired[sub, kind, low + SLOT : low + 2 * SLOT] = piece[at]


def second_terms_body(result, east, west, south, north, lens, coupling, earlier,
                      terms, vectors, kept, stacked):
    fill_multipliers(1, result, (east, west, south, north), lens, earlier, kept, vectors)
    coarse_terms(coupling, vectors, terms, stacked)


def terms_call(number, result, incoming, lens, coupling, extra):
    rows = result.shape[2]
    outs = [
        jax.ShapeDtypeStruct((2 * CORNERS, LANES), BF16),
        jax.ShapeDtypeStruct((2, 4 * rows, LANES), BF16),
        jax.ShapeDtypeStruct((2, 4 - 2 * number, rows, LANES), F32),
    ]
    if number == 0:
        outs.append(jax.ShapeDtypeStruct((2, 4, 2 * extra.shape[2], LANES), BF16))
    return pl.pallas_call(
        second_terms_body if number else first_terms_body,
        out_shape=outs,
        in_specs=[VMEM] * 8,
        out_specs=[VMEM] * len(outs),
        scratch_shapes=[pltpu.VMEM((2 * CORNERS, LANES), F32)],
        compiler_params=pltpu.CompilerParams(vmem_limit_bytes=SMALL_VMEM),
    )(result, *incoming, lens, coupling, extra)


def dual_body(flags, taut, wrinkle, vectors, result, east, west, south, north,
              unused, held, arrived):
    rows = result.shape[2]
    copies = loads_of(taut, wrinkle, held, arrived)
    start_loads(copies)
    product(copies, flags, held, vectors, result, (east, west, south, north), rows)


def correction_body(terms, select, paired, start, lens, out):
    rows = start.shape[2]
    solved = dot(select[...], terms[...]).astype(BF16)
    group = [solved[SLOT * k : SLOT * (k + 1)] for k in range(8)]
    other = {
        (0, EAST): group[1],
        (1, WEST): group[0],
        (0, NORTH): group[2],
        (1, NORTH): group[3],
        (0, SOUTH): group[4],
        (1, SOUTH): group[5],
        (0, WEST): group[6],
        (1, EAST): group[7],
    }
    for (sub, kind), values in other.items():
        stacked = jnp.concatenate([group[sub], -values], axis=0)
        for segment in range(paired.shape[2] // (2 * SLOT)):
            low = segment * LANES
            high = min(rows, low + LANES)
            both = paired[sub, kind, 2 * segment * SLOT : 2 * (segment + 1) * SLOT]
            shift = dot(both, stacked, ((0,), (0,)))[: high - low]
            spot = lax.broadcasted_iota(jnp.int32, (high - low, LANES), 0) + low
            live = spot.astype(F32) < lens[sub, kind, 0:1]
            out[sub, kind, low:high] = start[sub, kind, low:high] - jnp.where(
                live, 0.5 * shift, 0.0
            )


def correction_call(*operands):
    rows = operands[3].shape[2]
    return pl.pallas_call(
        correction_body,
        out_shape=jax.ShapeDtypeStruct((2, 4, rows, LANES), F32),
        in_specs=[VMEM] * len(operands),
        out_specs=VMEM,
        compiler_params=pltpu.CompilerParams(vmem_limit_bytes=SMALL_VMEM),
    )(*operands)


def residual_body(flags, taut, wrinkle, earlier, from_east, from_west, from_south, from_north,
                  lens, base, result, east, west, south, north, vectors, held, arrived):
    rows = earlier.shape[2]
    incoming = (from_east, from_west, from_south, from_north)
    copies = loads_of(taut, wrinkle, held, arrived)
    start_loads(copies)
    for sub in range(2):
        for kind in range(4):
            gap = preconditioned_part(earlier, incoming, lens, sub, kind, rows)
            vectors[sub, kind * rows : (kind + 1) * rows] = (base[sub, kind] - gap).astype(BF16)
    product(copies, flags, held, vectors, result, (east, west, south, north), rows)


def last_body(result, east, south, lens, out):
    rows = result.shape[2]
    for sub in range(2):
        for kind in range(2):
            out[sub, kind] = preconditioned_part(
                result, (east, None, south, None), lens, sub, kind, rows
            )


def coarse_rows(coarse_inverse, corner_map):
    row_count, col_count = coarse_inverse.shape
    rows_of = lax.axis_size("sx")
    cols_of = lax.axis_size("sy")
    per = 2 * CORNERS
    row_index = lax.axis_index("sx")
    tile_of = jnp.pad(corner_map.reshape(1, per), ((0, 7), (0, LANES - per)))
    row_maps = copies_of_all(tile_of, "sy")[:, 0, :per].reshape(cols_of * per)
    codes = jnp.concatenate([row_maps // 32, row_maps % 32]).astype(BF16)
    code_rows = codes.shape[0] // LANES
    tile = jnp.pad(coarse_inverse, ((0, 0), (0, LANES - col_count)))
    message = jnp.concatenate([tile, codes.reshape(code_rows, LANES)], axis=0)
    message = jnp.pad(message, ((0, 64 - message.shape[0]), (0, 0)))
    arrived = copies_of_all(message, "sx")
    columns = arrived[:, :row_count].reshape(rows_of * row_count, LANES)
    codes = arrived[:, row_count : row_count + code_rows].astype(jnp.int32)
    codes = codes.reshape(rows_of, 2, cols_of, per)
    maps = codes[:, 0] * 32 + codes[:, 1]
    at = lambda by: lax.dynamic_index_in_dim(maps, (row_index + by) % rows_of, 0, False)
    here, up, down = at(0), at(-1 + rows_of), at(1)
    groups = [
        here[:, :CORNERS],
        here[:, CORNERS:],
        up[:, :CORNERS],
        up[:, CORNERS:],
        down[:, :CORNERS],
        down[:, CORNERS:],
        jnp.roll(here, 1, axis=0)[:, CORNERS:],
        jnp.roll(here, -1, axis=0)[:, :CORNERS],
    ]
    wanted = jnp.pad(
        jnp.stack(groups, axis=1), ((0, 0), (0, 0), (0, SLOT - CORNERS)), constant_values=-1
    ).reshape(-1, 1)
    coarse_order = rows_of * row_count
    pick = (wanted == jnp.arange(coarse_order)[None]).astype(BF16)
    chosen = dot(pick, columns).astype(BF16).reshape(cols_of, -1, LANES)
    chosen = lax.all_to_all(chosen, "sy", 0, 0, tiled=True)
    flat = maps.reshape(-1)
    spot = (flat // col_count) * LANES + flat % col_count
    place = (jnp.arange(cols_of * LANES)[:, None] == spot[None]).astype(BF16)
    chosen = jnp.moveaxis(chosen, 0, 1).reshape(chosen.shape[1], -1)
    return dot(chosen, place).astype(BF16)


def steps(
    adjoint_loads,
    dual_taut,
    dual_wrinkle,
    dirichlet_taut,
    dirichlet_wrinkle,
    coupling,
    coarse_inverse,
    wrinkled,
    edge_lengths,
    corner_map,
):
    rows = adjoint_loads.shape[3]
    loads = adjoint_loads[0]
    flags = wrinkled[0]
    lengths = edge_lengths[0]
    spots = jnp.stack([lax.axis_index("sx"), lax.axis_index("sy")]).astype(jnp.int32)
    last = (2 * lax.axis_size("sy") - 1, lax.axis_size("sx") - 1)
    east, south = pl.pallas_call(
        functools.partial(pack_body, last),
        out_shape=[
            jax.ShapeDtypeStruct((1, rows + LEN_ROWS, LANES), BF16),
            jax.ShapeDtypeStruct((2, rows + LEN_ROWS, LANES), BF16),
        ],
        in_specs=[SMEM, SMEM, VMEM],
        out_specs=[VMEM] * 2,
        compiler_params=pltpu.CompilerParams(vmem_limit_bytes=SMALL_VMEM),
    )(spots, lengths, loads)
    _, from_left, _, from_up = exchanged((east, None, south, None))

    segments = -(-rows // LANES)
    pieces = coupling[0].reshape(2, CORNERS, 4, rows)
    pieces = jnp.pad(
        pieces, ((0, 0), (0, SLOT - CORNERS), (0, 0), (0, segments * LANES - rows))
    )
    pieces = pieces.reshape(2, SLOT, 4, segments, LANES)
    pieces = jnp.transpose(pieces, (0, 2, 3, 1, 4)).reshape(2, 4, segments * SLOT, LANES)
    select = coarse_rows(coarse_inverse, corner_map)

    result, *outgoing, lens, start = product_call(
        functools.partial(first_body, last), flags, dirichlet_taut, dirichlet_wrinkle,
        (spots, lengths, loads, from_left, from_up, pieces), [SMEM] * 2 + [VMEM] * 4,
        rows, segments * SLOT,
        (
            jax.ShapeDtypeStruct((2, 4, 8, LANES), F32),
            jax.ShapeDtypeStruct((2, 4, rows, LANES), F32),
        ),
    )
    for number in range(2):
        incoming = exchanged(outgoing)
        if number == 0:
            terms, vectors, kept, paired = terms_call(
                0, result, incoming, lens, coupling, pieces
            )
        else:
            terms, vectors, kept = terms_call(1, result, incoming, lens, coupling, kept)
        everyone = copies_of_all(terms, ("sx", "sy")).reshape(-1, LANES)
        result, *outgoing = product_call(
            dual_body, flags, dual_taut, dual_wrinkle, (vectors,), [VMEM], rows, 0
        )
        incoming = exchanged(outgoing)
        base = correction_call(everyone, select, paired, start, lens)
        result, *outgoing = product_call(
            residual_body, flags, dirichlet_taut, dirichlet_wrinkle,
            (result, *incoming, lens, base), [VMEM] * 7, rows, 0,
        )
    _, west, _, north = outgoing
    from_east, _, from_south, _ = exchanged((None, west, None, north))
    preconditioned = pl.pallas_call(
        last_body,
        out_shape=jax.ShapeDtypeStruct((2, 2, rows, LANES), F32),
        in_specs=[VMEM] * 4,
        out_specs=VMEM,
        compiler_params=pltpu.CompilerParams(vmem_limit_bytes=SMALL_VMEM),
    )(result, from_east, from_south, lens)
    return kept[None], preconditioned[None]


def solution(mesh):
    placed = (
        P("sx", "sy", None, None, None),
        P("sx", "sy", None, None),
        P("sx", "sy", None, None),
        P("sx", "sy", None, None),
        P("sx", "sy", None, None),
        P("sx", "sy", None, None),
        P("sx", "sy"),
        P("sx", "sy"),
        P("sx", "sy", None),
        P("sx", "sy", None),
    )
    return jax.shard_map(
        steps,
        mesh=mesh,
        in_specs=placed,
        out_specs=(P("sx", "sy", None, None, None), P("sx", "sy", None, None, None)),
        check_vma=False,
    )
```
